128 devices in a mesh: section: 8 (over y, core), dom: 16 (over z, x).
Axes of the slice: x: 4, y: 4, z: 4, core: 2. Of those that a mesh axis runs over, the one named last changes fastest.
Arguments:
- carry_h: bfloat16 [8, 16384, 512], P('section', 'dom'), may hold values from -6 to 6
- carry_h0: bfloat16 [8, 16384, 512], P('section', 'dom'), may hold values from -6 to 6
- new_h0: bfloat16 [3, 16384, 512], P(None, 'dom'), may hold values from -6 to 6
- weights: bfloat16 [8, 512, 512], P('section'), may hold values from -0.25 to 0.25
- adj_blocks: bfloat16 [128, 24, 128, 128], P('dom'), may hold values from -0.109375 to 0.109375
- col_index: int32 [128, 24], P('dom'), may hold values from 0 to 23
- counts: int32 [128], P('dom'), may hold values from 1 to 24, as said below
- send_list: int32 [16, 16], replicated, may hold values from 0 to 7
Outputs:
- layer_out: bfloat16 [8, 4, 16384, 512], P('section', None, 'dom')
The draws below stay inside these ranges and needn't reach their ends.
Inputs may be any that keep to these rules, and one draw needn't show every extreme that they name: `counts`: every graph part has a row block with exactly 24 live blocks; parts differ in their mean load.
All inputs are finite; a program needn't handle non-finite values.
Results may differ from the reference program's by a relative error of at most 0.0052.
Values may be sent and summed in bfloat16 or wider, within the bound.
A program may use at most 128 MiB of HBM per device.

```python
import math
import jax
import jax.numpy as jnp
from jax import lax

D = 512
ROWS_DEV = 1024
BLOCK = 128
SLOTS = 24
STEPS = 4
NEW_GROUPS = 3
GROUP = 16384
RBLOCKS = 128
TABLE = 24
N_SECTION = 8
N_DOM = 16


def draw_counts(key, part):
    per_part = ROWS_DEV // BLOCK
    total = per_part * N_DOM
    ceiling = jax.random.randint(jax.random.fold_in(key, 11), (N_DOM,), SLOTS // 2, SLOTS + 1)
    raw_draw = jax.random.randint(jax.random.fold_in(key, 12), (total,), 0, 1 << 20)
    owner_part = jnp.arange(total) // per_part
    drawn = 1 + raw_draw % ceiling[owner_part]
    chosen = jax.random.randint(jax.random.fold_in(key, 13), (N_DOM,), 0, per_part)
    full_row = jnp.arange(total) % per_part == chosen[owner_part]
    return jnp.where(full_row, SLOTS, drawn).astype(jnp.int32)


def set_ends(result, stream_key, least, largest):
    longest = result.shape.index(max(result.shape))
    spots = []
    for shift in (0, 1):
        where = [jax.random.randint(jax.random.fold_in(stream_key, axis), (), 0, length) for axis, length in enumerate(result.shape)]
        where[longest] = (where[longest] + shift) % result.shape[longest]
        spots.append(tuple(where))
    return result.at[spots[0]].set(least).at[spots[1]].set(largest)


def level_of(rng, shape, shards, low, top_value):
    def one(axis_at, shards_of):
        draws = jax.random.uniform(jax.random.fold_in(jax.random.fold_in(rng, 6), axis_at), (shards_of,), jnp.float32, low / len(shards), top_value / len(shards))
        return jnp.repeat(jnp.exp(draws), shape[axis_at] // shards_of).reshape((-1,) + (1,) * (len(shape) - axis_at - 1))

    level = one(*shards[0])
    for cut in shards[1:]:
        level = level * one(*cut)
    return level


def normal_values(own_key, dims, deviation, reach, cuts=(), kind=jnp.bfloat16):
    array = deviation * jax.random.normal(own_key, dims, jnp.float32)
    if cuts:
        array = array * level_of(own_key, dims, cuts, -0.22, 0.18)
    return jnp.clip(array, -reach, reach).astype(kind)


def setup_inputs(seed: int = 0) -> dict:
    keys = jax.random.split(jax.random.key(seed), 9)
    return {
        "carry_h": normal_values(keys[0], (N_SECTION, GROUP, D), 1.0, 6.0, ((0, 8), (1, 16))),
        "carry_h0": normal_values(keys[1], (N_SECTION, GROUP, D), 1.0, 6.0, ((0, 8), (1, 16))),
        "new_h0": normal_values(keys[2], (NEW_GROUPS, GROUP, D), 1.0, 6.0, ((1, 16),)),
        "weights": normal_values(keys[3], (N_SECTION, D, D), D ** -0.5, 0.25, ((0, 8),)),
        "adj_blocks": normal_values(keys[4], (RBLOCKS, SLOTS, BLOCK, BLOCK), (SLOTS * BLOCK) ** -0.5, 0.109375, ((0, 16),)),
        "col_index": set_ends(jax.random.randint(keys[5], (RBLOCKS, SLOTS), 0, TABLE), jax.random.fold_in(keys[5], 1), 0, TABLE - 1).astype(jnp.int32),
        "counts": draw_counts(jax.random.fold_in(keys[8], 71), 0),
        "send_list": set_ends(jax.random.randint(keys[7], (N_DOM, N_DOM), 0, ROWS_DEV // BLOCK), jax.random.fold_in(keys[7], 1), 0, (ROWS_DEV // BLOCK) - 1).astype(jnp.int32),
    }


teleport = 0.2
strength = 1.5


def apply_layer(current, anchor, weight, beta, adj_blocks, col_index, counts, send_list):
    per_part = ROWS_DEV // BLOCK
    blocks = current.reshape(N_DOM, per_part, BLOCK, D)
    incoming = blocks[jnp.arange(N_DOM)[None, :], send_list.T]
    tables = jnp.concatenate([blocks, incoming], axis=1)

    def row_block(inputs):
        adj_one, cols, live_count, row_id = inputs
        lookup = lax.dynamic_index_in_dim(tables, (row_id // per_part).astype(jnp.int32), 0, keepdims=False)
        picked = jnp.take(lookup, cols, axis=0)
        live_slots = jnp.arange(SLOTS) < live_count
        masked = jnp.where(live_slots[:, None, None], adj_one, jnp.zeros((), adj_one.dtype))
        return jnp.einsum("kij,kjd->id", masked.astype(jnp.float32), picked.astype(jnp.float32))

    row_ids = jnp.arange(RBLOCKS).astype(jnp.int32)
    gathered = lax.map(row_block, (adj_blocks, col_index, counts, row_ids)).reshape(GROUP, D)
    mixture = ((1.0 - teleport) * gathered + teleport * anchor.astype(jnp.float32)).astype(jnp.bfloat16)
    product = jnp.dot(mixture, weight, preferred_element_type=jnp.float32)
    return jax.nn.relu((1.0 - beta) * mixture.astype(jnp.float32) + beta * product).astype(jnp.bfloat16)


def reference(carry_h, carry_h0, new_h0, weights, adj_blocks, col_index, counts, send_list):
    history = []
    for step in range(STEPS):
        current_row = []
        for layer in range(N_SECTION):
            if step == 0:
                current = carry_h[layer]
            elif layer == 0:
                current = new_h0[step - 1]
            else:
                current = history[step - 1][layer - 1]
            if step <= layer:
                anchor = carry_h0[layer - step]
            else:
                anchor = new_h0[step - layer - 1]
            layer_beta = math.log(1.0 + strength / (layer + 1))
            current_row.append(apply_layer(current, anchor, weights[layer], layer_beta, adj_blocks, col_index, counts, send_list))
        history.append(current_row)
    return jnp.stack([jnp.stack([history[step][layer] for step in range(STEPS)]) for layer in range(N_SECTION)])
```

```python
import functools
import math

import jax
import jax.numpy as jnp
from jax import lax
from jax.experimental import pallas as pl
from jax.experimental.pallas import tpu as pltpu
from jax.sharding import PartitionSpec as P

BLOCK = 128
STEPS = 4
TELEPORT = 0.2
STRENGTH = 1.5
MESH = pl.DeviceIdType.MESH

ORDER = (
    (1, 1), (-1, -1),
    (1, -1), (-1, 1),
    (1, 2), (-1, 0),
    (1, 0), (-1, 2),
    (2, 2),
    (2, 0), (0, 2),
    (2, 1), (0, -1),
    (2, -1), (0, 1),
)
PEERS = len(ORDER)


def kernel(
    n_section, n_x, n_z,
    col, counts, send_list, betas, carry_h, carry_h0, new_h0, weights, adj,
    out,
    own0, own1, own2, own3, table0, table1, table2, table3, outgoing, held, result, adjacency, weight,
    token, load_sem, feed_sem, adj_sem, own_sem, send_sem, recv_sem, ship_send, ship_recv, held_send, held_recv, out_sem,
):
    section = lax.axis_index("section")
    part = lax.axis_index("dom")
    z, x = part // n_x, part % n_x
    core = section % 2
    owns = (own0, own1, own2, own3)
    tables = (table0, table1, table2, table3)
    blocks = own0.shape[0]
    pairs = blocks // 2
    slots = adj.shape[1]

    def at(dx, dz):
        return ((z + dz + n_z) % n_z) * n_x + (x + dx + n_x) % n_x

    def along(by):
        return {"section": (section + by + n_section) % n_section}

    barrier = pltpu.get_barrier_semaphore()
    for dx, dz in ORDER:
        pl.semaphore_signal(barrier, inc=1, device_id={"dom": at(dx, dz)}, device_id_type=MESH)
    for by in (1, -1, 2, -2):
        pl.semaphore_signal(barrier, inc=1, device_id=along(by), device_id_type=MESH)

    load_x = pltpu.make_async_copy(carry_h.at[0], own0, load_sem.at[0])
    load_held = pltpu.make_async_copy(carry_h0.at[0], held.at[0], load_sem.at[1])
    load_weight = pltpu.make_async_copy(weights.at[0], weight, load_sem.at[2])
    load_x.start()
    load_held.start()
    load_weight.start()

    def feed(t, what, target):
        return pltpu.make_async_copy(new_h0.at[t - 1], target, feed_sem.at[what, t])

    @pl.when(section == 0)
    def _():
        for t in range(1, STEPS):
            feed(t, 0, owns[t]).start()
            feed(t, 1, held.at[t]).start()

    load_adj = [
        pltpu.make_async_copy(
            adj.at[:, k], adjacency.at[:, k // 2, :, pl.ds((k % 2) * BLOCK, BLOCK)], adj_sem.at[k]
        )
        for k in range(slots)
    ]

    def exchange(t, j, owner):
        dx, dz = ORDER[j]
        return pltpu.make_async_remote_copy(
            src_ref=outgoing.at[t, j],
            dst_ref=tables[t].at[blocks + owner],
            send_sem=send_sem.at[t, j],
            recv_sem=recv_sem.at[t, j],
            device_id={"dom": at(dx, dz)},
            device_id_type=MESH,
        )

    def ship(t, g):
        rows = pl.ds(2 * g, 2)
        return pltpu.make_async_remote_copy(
            src_ref=result.at[t, rows],
            dst_ref=owns[t + 1].at[rows],
            send_sem=ship_send.at[t, g],
            recv_sem=ship_recv.at[t, g],
            device_id=along(1),
            device_id_type=MESH,
        )

    def leave(t, g):
        rows = pl.ds(2 * g, 2)
        return pltpu.make_async_copy(result.at[t, rows], out.at[t, rows], out_sem.at[t, g])

    def hand(n):
        source, target, by = ((0, 1, 1), (0, 2, 2), (1, 2, 1), (1, 3, 2), (2, 3, 1))[n]
        return pltpu.make_async_remote_copy(
            src_ref=held.at[source],
            dst_ref=held.at[target],
            send_sem=held_send.at[n],
            recv_sem=held_recv.at[target],
            device_id=along(by),
            device_id_type=MESH,
        )

    hands = (
        section < n_section - 1,
        (core == 0) & (section < n_section - 2),
        core == 0,
        (core == 0) & (section < n_section - 2),
        core == 0,
    )

    def own_to_table(t):
        return pltpu.make_async_copy(owns[t], tables[t].at[pl.ds(0, blocks)], own_sem.at[t])

    def send(t):
        if t == 0:
            load_x.wait()
        else:

            @pl.when(section == 0)
            def _():
                feed(t, 0, owns[t]).wait()

            @pl.when(section > 0)
            def _():
                for g in range(pairs):
                    ship(t - 1, g).wait_recv()

        own_to_table(t).start()
        for j, (dx, dz) in enumerate(ORDER):
            outgoing[t, j] = owns[t][send_list[part, at(dx, dz)]]
            if j:
                exchange(t, j - 1, part).start()
        tables[t][blocks + part] = owns[t][send_list[part, part]]
        exchange(t, PEERS - 1, part).start()

    def compute(t):
        if t > 0:

            @pl.when(section == 0)
            def _():
                feed(t, 1, held.at[t]).wait()

            @pl.when(section > 0)
            def _():
                hand((0, 0, 1, 3)[t]).wait_recv()

        for n in ((), (2, 3), (4,), ())[t]:

            @pl.when(hands[n])
            def _():
                hand(n).start()

        own_to_table(t).wait()
        for j, (dx, dz) in enumerate(ORDER):
            exchange(t, j, at(-dx, -dz)).wait_recv()
        beta = betas[section]

        def pair(g, carry):
            mixed = []
            for half in range(2):
                r = 2 * g + half
                total = None
                for k in range(slots // 2):
                    picked = jnp.concatenate(
                        [tables[t][col[r, 2 * k]], tables[t][col[r, 2 * k + 1]]], axis=0
                    )
                    term = jnp.dot(adjacency[r, k], picked, preferred_element_type=jnp.float32)
                    total = term if total is None else total + term
                anchor = held[t, r].astype(jnp.float32)
                mixed.append(((1.0 - TELEPORT) * total + TELEPORT * anchor).astype(jnp.bfloat16))
            mixture = jnp.concatenate(mixed, axis=0)
            product = jnp.dot(mixture, weight[...], preferred_element_type=jnp.float32)
            layer = (1.0 - beta) * mixture.astype(jnp.float32) + beta * product
            layer = jnp.maximum(layer, 0.0).astype(jnp.bfloat16)
            for half in range(2):
                result[t, 2 * g + half] = layer[half * BLOCK : (half + 1) * BLOCK]
            if t < STEPS - 1:

                @pl.when(section < n_section - 1)
                def _():
                    ship(t, g).start()

            leave(t, g).start()
            return carry

        lax.fori_loop(0, pairs, pair, 0)

    def on(which, *work):
        @pl.when(core == which)
        def _():
            for step, t in work:
                step(t)

    def pass_token(t):
        for j in range(PEERS):
            exchange(t, j, part).wait_send()
        pl.semaphore_signal(token, inc=1, device_id=along(1), device_id_type=MESH)

    def take_token(t):
        pl.semaphore_wait(token, 1)

    pl.semaphore_wait(barrier, PEERS + 4)
    on(0, (send, 0))

    for copy in load_adj:
        copy.start()
    load_held.wait()
    for n in (0, 1):

        @pl.when(hands[n])
        def _():
            hand(n).start()

    load_weight.wait()
    for copy in load_adj:
        copy.wait()

    def mask(r, carry):
        lane = lax.broadcasted_iota(jnp.int32, (BLOCK, 2 * BLOCK), 1)
        for k in range(slots // 2):
            live = lane < (counts[r] - 2 * k) * BLOCK
            adjacency[r, k] = jnp.where(live, adjacency[r, k], jnp.zeros((), jnp.bfloat16))
        return carry

    lax.fori_loop(0, blocks, mask, 0)

    on(0, (pass_token, 0), (compute, 0))
    on(1, (take_token, 0), (send, 0))
    send(1)
    on(0, (send, 2))
    on(1, (compute, 0))
    compute(1)
    on(0, (compute, 2))
    on(1, (send, 2))
    send(3)
    on(1, (compute, 2))
    compute(3)

    for t in range(STEPS):
        for g in range(pairs):
            leave(t, g).wait()
        if t:
            for j in range(PEERS):
                exchange(t, j, part).wait_send()

    @pl.when(core == 1)
    def _():
        for j in range(PEERS):
            exchange(0, j, part).wait_send()

    @pl.when(section < n_section - 1)
    def _():
        for t in range(STEPS - 1):
            for g in range(pairs):
                ship(t, g).wait_send()

    for n in range(len(hands)):

        @pl.when(hands[n])
        def _():
            hand(n).wait_send()


def solution(mesh):
    n_section, n_dom = mesh.shape["section"], mesh.shape["dom"]
    n_x = math.isqrt(n_dom)
    n_z = n_dom // n_x

    def body(carry_h, carry_h0, new_h0, weights, adj_blocks, col_index, counts, send_list):
        rows, width = carry_h.shape[1:]
        blocks, slots = adj_blocks.shape[:2]
        betas = jnp.asarray([math.log(1.0 + STRENGTH / (s + 1)) for s in range(n_section)], jnp.float32)
        tiles = (blocks, BLOCK, width)
        anywhere = pl.BlockSpec(memory_space=pl.ANY)
        scalars = pl.BlockSpec(memory_space=pltpu.SMEM)
        out = pl.pallas_call(
            functools.partial(kernel, n_section, n_x, n_z),
            out_shape=jax.ShapeDtypeStruct((STEPS, *tiles), jnp.bfloat16),
            in_specs=[scalars] * 4 + [anywhere] * 5,
            out_specs=anywhere,
            scratch_shapes=[pltpu.VMEM(tiles, jnp.bfloat16)] * STEPS
            + [pltpu.VMEM((blocks + n_dom, BLOCK, width), jnp.bfloat16)] * STEPS
            + [
                pltpu.VMEM((STEPS, PEERS, BLOCK, width), jnp.bfloat16),
                pltpu.VMEM((STEPS, *tiles), jnp.bfloat16),
                pltpu.VMEM((STEPS, *tiles), jnp.bfloat16),
                pltpu.VMEM((blocks, slots // 2, BLOCK, 2 * BLOCK), jnp.bfloat16),
                pltpu.VMEM((width, width), jnp.bfloat16),
                pltpu.SemaphoreType.REGULAR,
                pltpu.SemaphoreType.DMA((3,)),
                pltpu.SemaphoreType.DMA((2, STEPS)),
                pltpu.SemaphoreType.DMA((slots,)),
                pltpu.SemaphoreType.DMA((STEPS,)),
                pltpu.SemaphoreType.DMA((STEPS, PEERS)),
                pltpu.SemaphoreType.DMA((STEPS, PEERS)),
                pltpu.SemaphoreType.DMA((STEPS, blocks // 2)),
                pltpu.SemaphoreType.DMA((STEPS, blocks // 2)),
                pltpu.SemaphoreType.DMA((5,)),
                pltpu.SemaphoreType.DMA((STEPS,)),
                pltpu.SemaphoreType.DMA((STEPS, blocks // 2)),
            ],
            compiler_params=pltpu.CompilerParams(
                collective_id=0, has_side_effects=True, vmem_limit_bytes=62 << 20
            ),
        )(
            col_index, counts, send_list, betas,
            carry_h.reshape(1, *tiles), carry_h0.reshape(1, *tiles), new_h0.reshape(-1, *tiles), weights, adj_blocks,
        )
        return out.reshape(1, STEPS, rows, width)

    in_specs = (
        P("section", "dom", None),
        P("section", "dom", None),
        P(None, "dom", None),
        P("section", None, None),
        P("dom", None, None, None),
        P("dom", None),
        P("dom"),
        P(),
    )
    out_specs = P("section", None, "dom", None)
    return jax.shard_map(body, mesh=mesh, in_specs=in_specs, out_specs=out_specs, check_vma=False)
```

```python
import functools
import math

import jax
import jax.numpy as jnp
from jax import lax
from jax.experimental import pallas as pl
from jax.experimental.pallas import tpu as pltpu
from jax.sharding import PartitionSpec as P

BLOCK = 128
STEPS = 4
TELEPORT = 0.2
STRENGTH = 1.5
MESH = pl.DeviceIdType.MESH
HALVES = 2
CHUNKS = 4
PER = CHUNKS // HALVES

ORDER = (
    (1, 1), (-1, -1),
    (1, -1), (-1, 1),
    (1, 2), (-1, 0),
    (1, 0), (-1, 2),
    (2, 2),
    (2, 0), (0, 2),
    (2, 1), (0, -1),
    (2, -1), (0, 1),
)
PEERS = len(ORDER)
FIRST = 3


def kernel(n_section, n_x, n_z, col, counts, send_list, betas, carry_h, carry_h0, new_h0, weights, adj, out, *scratch):
    owns, scratch = [scratch[t * CHUNKS : (t + 1) * CHUNKS] for t in range(STEPS)], scratch[STEPS * CHUNKS :]
    tables, scratch = [scratch[t * HALVES : (t + 1) * HALVES] for t in range(STEPS)], scratch[STEPS * HALVES :]
    (
        outgoing, held, mixed, result, adjacency, weight,
        token, load_sem, feed_sem, adj_sem, own_sem, send_sem, recv_sem, ship_send, ship_recv, held_send, held_recv,
    ) = scratch
    section = lax.axis_index("section")
    part = lax.axis_index("dom")
    z, x = part // n_x, part % n_x
    core = section % 2
    blocks = held.shape[1]
    slots = adj.shape[1]
    wide = weight.shape[1] // CHUNKS
    half_wide = weight.shape[1] // HALVES

    def at(dx, dz):
        return ((z + dz + n_z) % n_z) * n_x + (x + dx + n_x) % n_x

    def along(by):
        return {"section": (section + by + n_section) % n_section}

    barrier = pltpu.get_barrier_semaphore()
    for dx, dz in ORDER:
        pl.semaphore_signal(barrier, inc=1, device_id={"dom": at(dx, dz)}, device_id_type=MESH)
    for by in (1, -1, 2, -2):
        pl.semaphore_signal(barrier, inc=1, device_id=along(by), device_id_type=MESH)

    def columns(c):
        return pl.ds(c * wide, wide)

    def load_x(c):
        return pltpu.make_async_copy(carry_h.at[0, :, :, columns(c)], owns[0][c], load_sem.at[0])

    load_held = pltpu.make_async_copy(carry_h0.at[0], held.at[0], load_sem.at[1])
    load_weight = pltpu.make_async_copy(weights.at[0], weight, load_sem.at[2])
    for c in range(CHUNKS):
        load_x(c).start()
    load_held.start()
    load_weight.start()

    def feed_x(t, c):
        return pltpu.make_async_copy(new_h0.at[t - 1, :, :, columns(c)], owns[t][c], feed_sem.at[0, t - 1])

    def feed_held(t):
        return pltpu.make_async_copy(new_h0.at[t - 1], held.at[t], feed_sem.at[1, t - 1])

    @pl.when(section == 0)
    def _():
        for t in range(1, STEPS):
            for c in range(CHUNKS):
                feed_x(t, c).start()
            feed_held(t).start()

    load_adj = [
        pltpu.make_async_copy(
            adj.at[:, k], adjacency.at[:, k // 2, :, pl.ds((k % 2) * BLOCK, BLOCK)], adj_sem
        )
        for k in range(slots)
    ]

    def exchange(t, c, j, owner):
        dx, dz = ORDER[j]
        return pltpu.make_async_remote_copy(
            src_ref=outgoing.at[t, c, j],
            dst_ref=tables[t][c // PER].at[c % PER, blocks + owner],
            send_sem=send_sem.at[STEPS if t == 0 and c >= FIRST else t],
            recv_sem=recv_sem.at[t, c // PER],
            device_id={"dom": at(dx, dz)},
            device_id_type=MESH,
        )

    def sent(n, first, count):
        part_of = outgoing.at[n % STEPS, pl.ds(first, count)]
        return pltpu.make_async_copy(part_of, part_of, send_sem.at[n])

    def arrived(t, h):
        part_of = tables[t][h].at[:, pl.ds(blocks, PEERS)]
        return pltpu.make_async_copy(part_of, part_of, recv_sem.at[t, h])

    def own_done(t, h):
        part_of = tables[t][h].at[:, pl.ds(0, blocks)]
        return pltpu.make_async_copy(part_of, part_of, own_sem.at[t, h])

    def ship(t, c):
        return pltpu.make_async_remote_copy(
            src_ref=result.at[t, c],
            dst_ref=owns[t + 1][c],
            send_sem=ship_send.at[t],
            recv_sem=ship_recv.at[t, c],
            device_id=along(1),
            device_id_type=MESH,
        )

    def hand(n):
        source, target, by = ((0, 1, 1), (0, 2, 2), (1, 2, 1), (1, 3, 2), (2, 3, 1))[n]
        return pltpu.make_async_remote_copy(
            src_ref=held.at[source],
            dst_ref=held.at[target],
            send_sem=held_send.at[n],
            recv_sem=held_recv.at[target],
            device_id=along(by),
            device_id_type=MESH,
        )

    hands = (
        section < n_section - 1,
        (core == 0) & (section < n_section - 2),
        core == 0,
        (core == 0) & (section < n_section - 2),
        core == 0,
    )

    def hand_on(n):
        @pl.when(hands[n])
        def _():
            hand(n).start()

    def own_to_table(t, c):
        return pltpu.make_async_copy(
            owns[t][c], tables[t][c // PER].at[c % PER, pl.ds(0, blocks)], own_sem.at[t, c // PER]
        )

    def send(t):
        if t == 0:
            pltpu.make_async_copy(held.at[0], held.at[0], load_sem.at[0]).wait()
        else:

            @pl.when(section == 0)
            def _():
                pltpu.make_async_copy(held.at[t], held.at[t], feed_sem.at[0, t - 1]).wait()

        for c in range(CHUNKS):
            if t:

                @pl.when(section > 0)
                def _():
                    ship(t - 1, c).wait_recv()

            own_to_table(t, c).start()
            for j, (dx, dz) in enumerate(ORDER):
                outgoing[t, c, j] = owns[t][c][send_list[part, at(dx, dz)]]
                if j:
                    exchange(t, c, j - 1, part).start()
            tables[t][c // PER][c % PER, blocks + part] = owns[t][c][send_list[part, part]]
            exchange(t, c, PEERS - 1, part).start()

    def wait_held(t):
        if t == 0:
            load_held.wait()
        else:

            @pl.when(section == 0)
            def _():
                feed_held(t).wait()

            @pl.when(section > 0)
            def _():
                hand((0, 0, 1, 3)[t]).wait_recv()

    def wait_table(t, h):
        own_done(t, h).wait()
        arrived(t, h).wait()

    def aggregate(t, h):
        table = tables[t][h]
        lanes = slice(h * half_wide, (h + 1) * half_wide)

        def entry(n):
            return jnp.concatenate([table[c, n] for c in range(PER)], axis=1)

        def rows(g, carry):
            for i in range(2):
                r = 2 * g + i
                total = None
                for k in range(slots // 2):
                    picked = jnp.concatenate([entry(col[r, 2 * k]), entry(col[r, 2 * k + 1])], axis=0)
                    term = jnp.dot(adjacency[r, k], picked, preferred_element_type=jnp.float32)
                    total = term if total is None else total + term
                anchor = held[t, r, :, lanes].astype(jnp.float32)
                mixed[r, :, lanes] = ((1.0 - TELEPORT) * total + TELEPORT * anchor).astype(jnp.bfloat16)
            return carry

        lax.fori_loop(0, blocks // 2, rows, 0)

    def finish(t):
        beta = betas[section]
        for h in range(HALVES):
            lanes = slice(h * half_wide, (h + 1) * half_wide)

            def rows(g, carry):
                mixture = jnp.concatenate([mixed[2 * g], mixed[2 * g + 1]], axis=0)
                product = jnp.dot(mixture, weight[:, lanes], preferred_element_type=jnp.float32)
                layer = (1.0 - beta) * mixture[:, lanes].astype(jnp.float32) + beta * product
                layer = jnp.maximum(layer, 0.0).astype(jnp.bfloat16)
                for i in range(2):
                    rows_of = layer[i * BLOCK : (i + 1) * BLOCK]
                    out[t, 2 * g + i, :, lanes] = rows_of
                    if t < STEPS - 1:
                        for c in range(PER):
                            result[t, h * PER + c, 2 * g + i] = rows_of[:, c * wide : (c + 1) * wide]
                return carry

            lax.fori_loop(0, blocks // 2, rows, 0)
            if t < STEPS - 1:

                @pl.when(section < n_section - 1)
                def _():
                    for c in range(h * PER, (h + 1) * PER):
                        ship(t, c).start()

    def let_in(n):
        @pl.when(section == 1)
        def _():
            pl.semaphore_signal(token.at[n], inc=1, device_id=along(-1), device_id_type=MESH)

    def first_half(t):
        if t:
            wait_held(t)
        wait_table(t, 0)
        if t == 1:
            let_in(1)
        aggregate(t, 0)

    def second_half(t):
        wait_table(t, 1)
        if t == 2:
            let_in(2)
        aggregate(t, 1)
        finish(t)

    def on(which, *work):
        @pl.when(core == which)
        def _():
            for step, t in work:
                step(t)

    def hold_back(n):
        @pl.when(section == 0)
        def _():
            pl.semaphore_wait(token.at[n], 1)

    def give_way(t):
        sent(0, 0, FIRST).wait()
        pl.semaphore_signal(token.at[0], inc=1, device_id=along(1), device_id_type=MESH)

    def take_turn(t):
        pl.semaphore_wait(token.at[0], 1)

    pl.semaphore_wait(barrier, PEERS + 4)
    on(0, (send, 0))

    for copy in load_adj:
        copy.start()
    load_held.wait()
    hand_on(0)
    load_weight.wait()
    pltpu.make_async_copy(adjacency, adjacency, adj_sem).wait()

    def mask(r, carry):
        lane = lax.broadcasted_iota(jnp.int32, (BLOCK, 2 * BLOCK), 1)
        for k in range(slots // 2):
            live = lane < (counts[r] - 2 * k) * BLOCK
            adjacency[r, k] = jnp.where(live, adjacency[r, k], jnp.zeros((), jnp.bfloat16))
        return carry

    lax.fori_loop(0, blocks, mask, 0)

    on(0, (give_way, 0))
    on(1, (take_turn, 0), (send, 0))
    on(1, (send, 1))
    first_half(0)
    hand_on(1)
    second_half(0)
    on(0, (hold_back, 1), (send, 1))

    @pl.when(section == 0)
    def _():
        send(2)

    first_half(1)
    hand_on(2)

    @pl.when((core == 0) & (section > 0))
    def _():
        send(2)

    second_half(1)
    hand_on(3)
    on(1, (send, 2), (send, 3))
    first_half(2)
    hand_on(4)
    second_half(2)
    on(0, (hold_back, 2), (send, 3))
    first_half(3)
    second_half(3)

    @pl.when(core == 1)
    def _():
        sent(0, 0, FIRST).wait()

    sent(STEPS, FIRST, CHUNKS - FIRST).wait()
    for t in range(1, STEPS):
        sent(t, 0, CHUNKS).wait()

    @pl.when(section < n_section - 1)
    def _():
        for t in range(STEPS - 1):
            pltpu.make_async_copy(result.at[t], result.at[t], ship_send.at[t]).wait()

    for n in range(len(hands)):

        @pl.when(hands[n])
        def _():
            hand(n).wait_send()


def solution(mesh):
    n_section, n_dom = mesh.shape["section"], mesh.shape["dom"]
    n_x = math.isqrt(n_dom)
    n_z = n_dom // n_x

    def body(carry_h, carry_h0, new_h0, weights, adj_blocks, col_index, counts, send_list):
        rows, width = carry_h.shape[1:]
        blocks, slots = adj_blocks.shape[:2]
        wide = width // CHUNKS
        betas = jnp.asarray([math.log(1.0 + STRENGTH / (s + 1)) for s in range(n_section)], jnp.float32)
        tiles = (blocks, BLOCK, width)
        anywhere = pl.BlockSpec(memory_space=pltpu.HBM)
        scalars = pl.BlockSpec(memory_space=pltpu.SMEM)
        vmem = lambda *shape: pltpu.VMEM(shape, jnp.bfloat16)
        dma = lambda *shape: pltpu.SemaphoreType.DMA(shape)
        out = pl.pallas_call(
            functools.partial(kernel, n_section, n_x, n_z),
            out_shape=vmem(STEPS, *tiles),
            in_specs=[scalars] * 4 + [anywhere] * 5,
            out_specs=pl.BlockSpec(memory_space=pltpu.VMEM),
            scratch_shapes=[vmem(blocks, BLOCK, wide)] * (STEPS * CHUNKS)
            + [vmem(PER, blocks + n_dom, BLOCK, wide)] * (STEPS * HALVES)
            + [
                vmem(STEPS, CHUNKS, PEERS, BLOCK, wide),
                vmem(STEPS, *tiles),
                vmem(*tiles),
                vmem(STEPS - 1, CHUNKS, blocks, BLOCK, wide),
                vmem(blocks, slots // 2, BLOCK, 2 * BLOCK),
                vmem(width, width),
                pltpu.SemaphoreType.REGULAR((3,)),
                dma(3),
                dma(2, STEPS - 1),
                pltpu.SemaphoreType.DMA,
                dma(STEPS, HALVES),
                dma(STEPS + 1),
                dma(STEPS, HALVES),
                dma(STEPS - 1),
                dma(STEPS - 1, CHUNKS),
                dma(5),
                dma(STEPS),
            ],
            compiler_params=pltpu.CompilerParams(
                collective_id=0, has_side_effects=True, vmem_limit_bytes=67_043_328 - (4 << 20) - (64 << 10)
            ),
        )(
            col_index, counts, send_list, betas,
            carry_h.reshape(1, *tiles), carry_h0.reshape(1, *tiles), new_h0.reshape(-1, *tiles), weights, adj_blocks,
        )
        return out.reshape(1, STEPS, rows, width)

    in_specs = (
        P("section", "dom", None),
        P("section", "dom", None),
        P(None, "dom", None),
        P("section", None, None),
        P("dom", None, None, None),
        P("dom", None),
        P("dom"),
        P(),
    )
    out_specs = P("section", None, "dom", None)
    return jax.shard_map(body, mesh=mesh, in_specs=in_specs, out_specs=out_specs, check_vma=False)
```

```python
import functools
import math

import jax
import jax.numpy as jnp
from jax import lax
from jax.experimental import pallas as pl
from jax.experimental.pallas import tpu as pltpu
from jax.sharding import PartitionSpec as P

BLOCK = 128
STEPS = 4
TELEPORT = 0.2
STRENGTH = 1.5
MESH = pl.DeviceIdType.MESH
CHUNKS = 4
HALVES = 2
PER = CHUNKS // HALVES

ORDER = (
    (2, 2),
    (2, 1), (0, -1),
    (2, -1), (0, 1),
    (1, 2), (-1, 0),
    (1, 0), (-1, 2),
    (1, 1), (-1, -1),
    (1, -1), (-1, 1),
    (2, 0), (0, 2),
)
PEERS = len(ORDER)
FIRST = 3


def kernel(n_section, n_x, n_z, col, counts, send_list, betas, carry_h, carry_h0, new_h0, weights, adj, out, *scratch):
    owns, scratch = [scratch[t * CHUNKS : (t + 1) * CHUNKS] for t in range(STEPS)], scratch[STEPS * CHUNKS :]
    tables, scratch = [scratch[t * HALVES : (t + 1) * HALVES] for t in range(STEPS)], scratch[STEPS * HALVES :]
    (
        outgoing, held, partial, result, adjacency, weight,
        token, load_sem, feed_sem, adj_sem, own_sem, send_sem, recv_sem, ship_send, ship_recv, held_send, held_recv,
    ) = scratch
    section = lax.axis_index("section")
    part = lax.axis_index("dom")
    z, x = part // n_x, part % n_x
    core = section % 2
    blocks = held.shape[1]
    slots = adj.shape[1]
    wide = weight.shape[1] // CHUNKS
    half = PER * wide

    def at(dx, dz):
        return ((z + dz + n_z) % n_z) * n_x + (x + dx + n_x) % n_x

    def along(by):
        return {"section": (section + by + n_section) % n_section}

    barrier = pltpu.get_barrier_semaphore()
    for dx, dz in ORDER:
        pl.semaphore_signal(barrier, inc=1, device_id={"dom": at(dx, dz)}, device_id_type=MESH)
    for by in (1, -1, 2, -2):
        pl.semaphore_signal(barrier, inc=1, device_id=along(by), device_id_type=MESH)

    def columns(c):
        return pl.ds(c * wide, wide)

    def load_x(c):
        return pltpu.make_async_copy(carry_h.at[0, :, :, columns(c)], owns[0][c], load_sem.at[0])

    load_held = pltpu.make_async_copy(carry_h0.at[0], held.at[0], load_sem.at[1])
    load_weight = pltpu.make_async_copy(weights.at[0], weight, load_sem.at[2])
    for c in range(CHUNKS):
        load_x(c).start()
    load_held.start()
    load_weight.start()

    def feed_x(t, c):
        return pltpu.make_async_copy(new_h0.at[t - 1, :, :, columns(c)], owns[t][c], feed_sem.at[0, t - 1])

    def feed_held(t):
        return pltpu.make_async_copy(new_h0.at[t - 1], held.at[t], feed_sem.at[1, t - 1])

    @pl.when(section == 0)
    def _():
        for t in range(1, STEPS):
            for c in range(CHUNKS):
                feed_x(t, c).start()
            feed_held(t).start()

    load_adj = [
        pltpu.make_async_copy(
            adj.at[:, k], adjacency.at[:, k // 2, :, pl.ds((k % 2) * BLOCK, BLOCK)], adj_sem
        )
        for k in range(slots)
    ]

    def exchange(t, c, j, owner):
        dx, dz = ORDER[j]
        return pltpu.make_async_remote_copy(
            src_ref=outgoing.at[t, c, j],
            dst_ref=tables[t][c // PER].at[c % PER, blocks + owner],
            send_sem=send_sem.at[STEPS if t == 0 and c >= FIRST else t],
            recv_sem=recv_sem.at[t, c // PER],
            device_id={"dom": at(dx, dz)},
            device_id_type=MESH,
        )

    def sent(n, first, count):
        part_of = outgoing.at[n % STEPS, pl.ds(first, count)]
        return pltpu.make_async_copy(part_of, part_of, send_sem.at[n])

    def arrived(t, h):
        part_of = tables[t][h].at[:, pl.ds(blocks, PEERS)]
        return pltpu.make_async_copy(part_of, part_of, recv_sem.at[t, h])

    def own_done(t, h):
        part_of = tables[t][h].at[:, pl.ds(0, blocks)]
        return pltpu.make_async_copy(part_of, part_of, own_sem.at[t, h])

    def ship(t, c, first, count):
        rows = pl.ds(first, count)
        return pltpu.make_async_remote_copy(
            src_ref=result.at[t, c, rows],
            dst_ref=owns[t + 1][c].at[rows],
            send_sem=ship_send.at[t],
            recv_sem=ship_recv.at[t, c],
            device_id=along(1),
            device_id_type=MESH,
        )

    def hand(n):
        source, target, by = ((0, 1, 1), (0, 2, 2), (1, 2, 1), (1, 3, 2), (2, 3, 1))[n]
        return pltpu.make_async_remote_copy(
            src_ref=held.at[source],
            dst_ref=held.at[target],
            send_sem=held_send.at[n],
            recv_sem=held_recv.at[target],
            device_id=along(by),
            device_id_type=MESH,
        )

    hands = (
        section < n_section - 1,
        (core == 0) & (section < n_section - 2),
        core == 0,
        (core == 0) & (section < n_section - 2),
        core == 0,
    )

    def hand_on(n):
        @pl.when(hands[n])
        def _():
            hand(n).start()

    def own_to_table(t, c):
        return pltpu.make_async_copy(
            owns[t][c], tables[t][c // PER].at[c % PER, pl.ds(0, blocks)], own_sem.at[t, c // PER]
        )

    def send(t, chunks=range(CHUNKS)):
        if 0 not in chunks:
            pass
        elif t == 0:
            pltpu.make_async_copy(held.at[0], held.at[0], load_sem.at[0]).wait()
        else:

            @pl.when(section == 0)
            def _():
                pltpu.make_async_copy(held.at[t], held.at[t], feed_sem.at[0, t - 1]).wait()

        for c in chunks:
            if t:

                @pl.when(section > 0)
                def _():
                    ship(t - 1, c, 0, blocks).wait_recv()

            own_to_table(t, c).start()
            for j, (dx, dz) in enumerate(ORDER):
                outgoing[t, c, j] = owns[t][c][send_list[part, at(dx, dz)]]
                if j:
                    exchange(t, c, j - 1, part).start()
            tables[t][c // PER][c % PER, blocks + part] = owns[t][c][send_list[part, part]]
            exchange(t, c, PEERS - 1, part).start()

    def wait_held(t):
        if t == 0:
            load_held.wait()
        else:

            @pl.when(section == 0)
            def _():
                feed_held(t).wait()

            @pl.when(section > 0)
            def _():
                hand((0, 0, 1, 3)[t]).wait_recv()

    def wait_table(t, h):
        own_done(t, h).wait()
        arrived(t, h).wait()

    def mix(t, h, r):
        table = tables[t][h]

        def entry(n):
            return jnp.concatenate([table[c, n] for c in range(PER)], axis=1)

        total = None
        for k in range(slots // 2):
            picked = jnp.concatenate([entry(col[r, 2 * k]), entry(col[r, 2 * k + 1])], axis=0)
            term = jnp.dot(adjacency[r, k], picked, preferred_element_type=jnp.float32)
            total = term if total is None else total + term
        anchor = held[t, r, :, h * half : (h + 1) * half].astype(jnp.float32)
        return ((1.0 - TELEPORT) * total + TELEPORT * anchor).astype(jnp.bfloat16)

    def begin(t):
        beta = betas[section]

        def rows(g, carry):
            left = jnp.concatenate([mix(t, 0, 2 * g), mix(t, 0, 2 * g + 1)], axis=0)
            product = beta * jnp.dot(left, weight[:half], preferred_element_type=jnp.float32)
            partial[g, :, :half] = product[:, :half] + (1.0 - beta) * left.astype(jnp.float32)
            partial[g, :, half:] = product[:, half:]
            return carry

        lax.fori_loop(0, blocks // 2, rows, 0)

    def finish(t):
        beta = betas[section]

        def rows(g, carry):
            right = jnp.concatenate([mix(t, 1, 2 * g), mix(t, 1, 2 * g + 1)], axis=0)
            layer = partial[g] + beta * jnp.dot(right, weight[half:], preferred_element_type=jnp.float32)
            layer = jnp.concatenate(
                [layer[:, :half], layer[:, half:] + (1.0 - beta) * right.astype(jnp.float32)], axis=1
            )
            layer = jnp.maximum(layer, 0.0).astype(jnp.bfloat16)
            for i in range(2):
                rows_of = layer[i * BLOCK : (i + 1) * BLOCK]
                out[t, 2 * g + i] = rows_of
                if t < STEPS - 1:
                    for c in range(CHUNKS):
                        result[t, c, 2 * g + i] = rows_of[:, c * wide : (c + 1) * wide]
            if t < STEPS - 1:

                @pl.when(section < n_section - 1)
                def _():
                    ship(t, 0, 2 * g, 2).start()

            return carry

        lax.fori_loop(0, blocks // 2, rows, 0)
        if t < STEPS - 1:

            @pl.when(section < n_section - 1)
            def _():
                for c in range(1, CHUNKS):
                    ship(t, c, 0, blocks).start()

    def let_in(n):
        @pl.when(section == 1)
        def _():
            pl.semaphore_signal(token.at[n], inc=1, device_id=along(-1), device_id_type=MESH)

    def first_half(t):
        if t:
            wait_held(t)
        wait_table(t, 0)
        if t == 1:
            let_in(1)
        begin(t)

    def second_half(t):
        wait_table(t, 1)
        if t == 2:
            let_in(2)
        finish(t)

    def on(which, *work):
        @pl.when(core == which)
        def _():
            for step, t in work:
                step(t)

    def hold_back(n):
        @pl.when(section == 0)
        def _():
            pl.semaphore_wait(token.at[n], 1)

    def give_way(t):
        sent(0, 0, FIRST).wait()
        pl.semaphore_signal(token.at[0], inc=1, device_id=along(1), device_id_type=MESH)

    def take_turn(t):
        pl.semaphore_wait(token.at[0], 1)

    pl.semaphore_wait(barrier, PEERS + 4)
    on(0, (send, 0))

    for copy in load_adj:
        copy.start()
    load_held.wait()
    hand_on(0)
    load_weight.wait()
    pltpu.make_async_copy(adjacency, adjacency, adj_sem).wait()

    def mask(r, carry):
        lane = lax.broadcasted_iota(jnp.int32, (BLOCK, 2 * BLOCK), 1)
        for k in range(slots // 2):
            live = lane < (counts[r] - 2 * k) * BLOCK
            adjacency[r, k] = jnp.where(live, adjacency[r, k], jnp.zeros((), jnp.bfloat16))
        return carry

    lax.fori_loop(0, blocks, mask, 0)

    on(0, (give_way, 0))
    on(1, (take_turn, 0), (send, 0))
    on(1, (send, 1))
    first_half(0)
    hand_on(1)
    second_half(0)
    on(0, (hold_back, 1), (send, 1))

    @pl.when(section == 0)
    def _():
        send(2)

    first_half(1)
    hand_on(2)

    @pl.when((core == 0) & (section > 0))
    def _():
        send(2, (0, 1, 2))

    second_half(1)

    @pl.when((core == 0) & (section > 0))
    def _():
        send(2, (3,))

    hand_on(3)
    on(1, (send, 2), (send, 3))
    first_half(2)
    hand_on(4)
    second_half(2)
    on(0, (hold_back, 2), (send, 3))
    first_half(3)
    second_half(3)

    @pl.when(core == 1)
    def _():
        sent(0, 0, FIRST).wait()

    sent(STEPS, FIRST, CHUNKS - FIRST).wait()
    for t in range(1, STEPS):
        sent(t, 0, CHUNKS).wait()

    @pl.when(section < n_section - 1)
    def _():
        for t in range(STEPS - 1):
            pltpu.make_async_copy(result.at[t], result.at[t], ship_send.at[t]).wait()

    for n in range(len(hands)):

        @pl.when(hands[n])
        def _():
            hand(n).wait_send()


def solution(mesh):
    n_section, n_dom = mesh.shape["section"], mesh.shape["dom"]
    n_x = math.isqrt(n_dom)
    n_z = n_dom // n_x

    def body(carry_h, carry_h0, new_h0, weights, adj_blocks, col_index, counts, send_list):
        rows, width = carry_h.shape[1:]
        blocks, slots = adj_blocks.shape[:2]
        wide = width // CHUNKS
        betas = jnp.asarray([math.log(1.0 + STRENGTH / (s + 1)) for s in range(n_section)], jnp.float32)
        tiles = (blocks, BLOCK, width)
        anywhere = pl.BlockSpec(memory_space=pltpu.HBM)
        scalars = pl.BlockSpec(memory_space=pltpu.SMEM)
        vmem = lambda *shape: pltpu.VMEM(shape, jnp.bfloat16)
        dma = lambda *shape: pltpu.SemaphoreType.DMA(shape)
        out = pl.pallas_call(
            functools.partial(kernel, n_section, n_x, n_z),
            out_shape=vmem(STEPS, *tiles),
            in_specs=[scalars] * 4 + [anywhere] * 5,
            out_specs=pl.BlockSpec(memory_space=pltpu.VMEM),
            scratch_shapes=[vmem(blocks, BLOCK, wide)] * (STEPS * CHUNKS)
            + [vmem(PER, blocks + n_dom, BLOCK, wide)] * (STEPS * HALVES)
            + [
                vmem(STEPS, CHUNKS, PEERS, BLOCK, wide),
                vmem(STEPS, *tiles),
                pltpu.VMEM((blocks // 2, 2 * BLOCK, width), jnp.float32),
                vmem(STEPS - 1, CHUNKS, blocks, BLOCK, wide),
                vmem(blocks, slots // 2, BLOCK, 2 * BLOCK),
                vmem(width, width),
                pltpu.SemaphoreType.REGULAR((3,)),
                dma(3),
                dma(2, STEPS - 1),
                pltpu.SemaphoreType.DMA,
                dma(STEPS, HALVES),
                dma(STEPS + 1),
                dma(STEPS, HALVES),
                dma(STEPS - 1),
                dma(STEPS - 1, CHUNKS),
                dma(5),
                dma(STEPS),
            ],
            compiler_params=pltpu.CompilerParams(
                collective_id=0, has_side_effects=True, vmem_limit_bytes=67_043_328 - (4 << 20) - (64 << 10)
            ),
        )(
            col_index, counts, send_list, betas,
            carry_h.reshape(1, *tiles), carry_h0.reshape(1, *tiles), new_h0.reshape(-1, *tiles), weights, adj_blocks,
        )
        return out.reshape(1, STEPS, rows, width)

    in_specs = (
        P("section", "dom", None),
        P("section", "dom", None),
        P(None, "dom", None),
        P("section", None, None),
        P("dom", None, None, None),
        P("dom", None),
        P("dom"),
        P(),
    )
    out_specs = P("section", None, "dom", None)
    return jax.shard_map(body, mesh=mesh, in_specs=in_specs, out_specs=out_specs, check_vma=False)
```

```python
import functools
import math

import jax
import jax.numpy as jnp
from jax import lax
from jax.experimental import pallas as pl
from jax.experimental.pallas import tpu as pltpu
from jax.sharding import PartitionSpec as P

BLOCK = 128
STEPS = 4
TELEPORT = 0.2
STRENGTH = 1.5
MESH = pl.DeviceIdType.MESH
CHUNKS = 4
HALVES = 2
PER = CHUNKS // HALVES

ORDER = (
    (2, 2),
    (2, 1), (1, 2), (2, -1), (-1, 2),
    (1, 1), (-1, -1),
    (1, -1), (-1, 1),
    (2, 0), (0, 2),
    (1, 0), (-1, 0), (0, 1), (0, -1),
)
PEERS = len(ORDER)
FIRST = 3


def beta_at(layer):
    return math.log(1.0 + STRENGTH / (layer + 1))


def kernel(n_section, n_x, n_z, col, counts, send_list, carry_h, carry_h0, new_h0, weights, adj, out, *scratch):
    owns, scratch = [scratch[t * CHUNKS : (t + 1) * CHUNKS] for t in range(STEPS)], scratch[STEPS * CHUNKS :]
    tables, scratch = [scratch[t * HALVES : (t + 1) * HALVES] for t in range(STEPS)], scratch[STEPS * HALVES :]
    (
        outgoing, held, partial, lines, result, adjacency, weight,
        token, load_sem, feed_sem, adj_sem, own_sem, send_sem, recv_sem, ship_send, ship_recv, held_send, held_recv,
    ) = scratch
    section = lax.axis_index("section")
    part = lax.axis_index("dom")
    z, x = part // n_x, part % n_x
    core = section % 2
    blocks = held.shape[1]
    slots = adj.shape[1]
    wide = weight.shape[1] // CHUNKS
    half = PER * wide

    def at(dx, dz):
        return ((z + dz + n_z) % n_z) * n_x + (x + dx + n_x) % n_x

    def along(by):
        return {"section": (section + by + n_section) % n_section}

    barrier = pltpu.get_barrier_semaphore()
    for dx, dz in ORDER:
        pl.semaphore_signal(barrier, inc=1, device_id={"dom": at(dx, dz)}, device_id_type=MESH)
    for by in (1, -1, 2, -2):
        pl.semaphore_signal(barrier, inc=1, device_id=along(by), device_id_type=MESH)

    def columns(c):
        return pl.ds(c * wide, wide)

    def load_x(c):
        return pltpu.make_async_copy(carry_h.at[0, :, :, columns(c)], owns[0][c], load_sem.at[0])

    load_held = pltpu.make_async_copy(carry_h0.at[0], held.at[0], load_sem.at[1])
    load_weight = pltpu.make_async_copy(weights.at[0], weight, load_sem.at[2])
    for c in range(CHUNKS):
        load_x(c).start()
    load_held.start()
    load_weight.start()

    def feed_x(t, c):
        return pltpu.make_async_copy(new_h0.at[t - 1, :, :, columns(c)], owns[t][c], feed_sem.at[0, t - 1])

    def feed_held(t):
        return pltpu.make_async_copy(new_h0.at[t - 1], held.at[t], feed_sem.at[1, t - 1])

    @pl.when(section == 0)
    def _():
        for t in range(1, STEPS):
            for c in range(CHUNKS):
                feed_x(t, c).start()
            feed_held(t).start()

    load_adj = [
        pltpu.make_async_copy(
            adj.at[:, k], adjacency.at[:, k // 2, :, pl.ds((k % 2) * BLOCK, BLOCK)], adj_sem
        )
        for k in range(slots)
    ]

    def exchange(t, c, j, owner):
        dx, dz = ORDER[j]
        return pltpu.make_async_remote_copy(
            src_ref=outgoing.at[t, c, j],
            dst_ref=tables[t][c // PER].at[c % PER, blocks + owner],
            send_sem=send_sem.at[t, int(c >= FIRST)],
            recv_sem=recv_sem.at[t, c // PER],
            device_id={"dom": at(dx, dz)},
            device_id_type=MESH,
        )

    def sent(t, late):
        part_of = outgoing.at[t, pl.ds(FIRST, CHUNKS - FIRST) if late else pl.ds(0, FIRST)]
        return pltpu.make_async_copy(part_of, part_of, send_sem.at[t, late])

    def arrived(t, h):
        part_of = tables[t][h].at[:, pl.ds(blocks, PEERS)]
        return pltpu.make_async_copy(part_of, part_of, recv_sem.at[t, h])

    def own_done(t, h):
        part_of = tables[t][h].at[:, pl.ds(0, blocks)]
        return pltpu.make_async_copy(part_of, part_of, own_sem.at[t, h])

    def ship(t, c, first, count):
        rows = pl.ds(first, count)
        return pltpu.make_async_remote_copy(
            src_ref=result.at[t, c, rows],
            dst_ref=owns[t + 1][c].at[rows],
            send_sem=ship_send.at[t],
            recv_sem=ship_recv.at[t, c],
            device_id=along(1),
            device_id_type=MESH,
        )

    def hand(n):
        source, target, by = ((0, 1, 1), (0, 2, 2), (1, 2, 1), (1, 3, 2), (2, 3, 1))[n]
        return pltpu.make_async_remote_copy(
            src_ref=held.at[source],
            dst_ref=held.at[target],
            send_sem=held_send.at[n],
            recv_sem=held_recv.at[target],
            device_id=along(by),
            device_id_type=MESH,
        )

    hands = (
        section < n_section - 1,
        (core == 0) & (section < n_section - 2),
        core == 0,
        (core == 0) & (section < n_section - 2),
        core == 0,
    )

    def hand_on(n):
        @pl.when(hands[n])
        def _():
            hand(n).start()

    def own_to_table(t, c):
        return pltpu.make_async_copy(
            owns[t][c], tables[t][c // PER].at[c % PER, pl.ds(0, blocks)], own_sem.at[t, c // PER]
        )

    def send(t, chunks=range(CHUNKS)):
        if 0 not in chunks:
            pass
        elif t == 0:
            pltpu.make_async_copy(held.at[0], held.at[0], load_sem.at[0]).wait()
        else:

            @pl.when(section == 0)
            def _():
                pltpu.make_async_copy(held.at[t], held.at[t], feed_sem.at[0, t - 1]).wait()

        for c in chunks:
            if t:

                @pl.when(section > 0)
                def _():
                    ship(t - 1, c, 0, blocks).wait_recv()

            own_to_table(t, c).start()
            for j, (dx, dz) in enumerate(ORDER):
                outgoing[t, c, j] = owns[t][c][send_list[part, at(dx, dz)]]
                if j:
                    exchange(t, c, j - 1, part).start()
            tables[t][c // PER][c % PER, blocks + part] = owns[t][c][send_list[part, part]]
            exchange(t, c, PEERS - 1, part).start()

    def wait_held(t):
        if t == 0:
            load_held.wait()
        else:

            @pl.when(section == 0)
            def _():
                feed_held(t).wait()

            @pl.when(section > 0)
            def _():
                hand((0, 0, 1, 3)[t]).wait_recv()

    def wait_table(t, h):
        own_done(t, h).wait()
        arrived(t, h).wait()

    def beta_of():
        value = jnp.float32(beta_at(n_section - 1))
        for s in range(n_section - 1):
            value = jnp.where(section == s, jnp.float32(beta_at(s)), value)
        return value

    def mix(t, h, r):
        table = tables[t][h]

        def entry(n):
            return jnp.concatenate([table[c, n] for c in range(PER)], axis=1)

        total = None
        for k in range(slots // 2):
            picked = jnp.concatenate([entry(col[r, 2 * k]), entry(col[r, 2 * k + 1])], axis=0)
            term = jnp.dot(adjacency[r, k], picked, preferred_element_type=jnp.float32)
            total = term if total is None else total + term
        anchor = held[t, r, :, h * half : (h + 1) * half].astype(jnp.float32)
        return ((1.0 - TELEPORT) * total + TELEPORT * anchor).astype(jnp.bfloat16)

    def pipelined(t, h, use, after=lambda g: None):
        def gather(g):
            lines[g] = jnp.concatenate([mix(t, h, 2 * g), mix(t, h, 2 * g + 1)], axis=0)

        def rows(g, carry):
            use(g - 1, lines[g - 1])
            gather(g)
            after(g - 1)
            return carry

        gather(0)
        lax.fori_loop(1, blocks // 2, rows, 0)
        use(blocks // 2 - 1, lines[blocks // 2 - 1])
        after(blocks // 2 - 1)

    def begin(t):
        beta = beta_of()

        def use(g, left):
            product = beta * jnp.dot(left, weight[:half], preferred_element_type=jnp.float32)
            partial[g, :, :half] = product[:, :half] + (1.0 - beta) * left.astype(jnp.float32)
            partial[g, :, half:] = product[:, half:]

        pipelined(t, 0, use)

    def finish(t):
        beta = beta_of()

        def use(g, right):
            layer = partial[g] + beta * jnp.dot(right, weight[half:], preferred_element_type=jnp.float32)
            layer = jnp.concatenate(
                [layer[:, :half], layer[:, half:] + (1.0 - beta) * right.astype(jnp.float32)], axis=1
            )
            layer = jnp.maximum(layer, 0.0).astype(jnp.bfloat16)
            for i in range(2):
                rows_of = layer[i * BLOCK : (i + 1) * BLOCK]
                out[t, 2 * g + i] = rows_of
                if t < STEPS - 1:
                    for c in range(CHUNKS):
                        result[t, c, 2 * g + i] = rows_of[:, c * wide : (c + 1) * wide]

        def after(g):
            if t < STEPS - 1:

                @pl.when(section < n_section - 1)
                def _():
                    ship(t, 0, 2 * g, 2).start()

        pipelined(t, 1, use, after)
        if t < STEPS - 1:

            @pl.when(section < n_section - 1)
            def _():
                for c in range(1, CHUNKS):
                    ship(t, c, 0, blocks).start()

    def let_in(n):
        @pl.when(section == 1)
        def _():
            pl.semaphore_signal(token.at[n], inc=1, device_id=along(-1), device_id_type=MESH)

    def first_half(t):
        if t:
            wait_held(t)
        wait_table(t, 0)
        if t == 1:
            let_in(1)
        begin(t)

    def second_half(t):
        wait_table(t, 1)
        if t == 2:
            let_in(2)
        finish(t)

    def on(which, *work):
        @pl.when(core == which)
        def _():
            for step, t in work:
                step(t)

    def hold_back(n):
        @pl.when(section == 0)
        def _():
            pl.semaphore_wait(token.at[n], 1)

    def give_way(t):
        sent(0, 0).wait()
        pl.semaphore_signal(token.at[0], inc=1, device_id=along(1), device_id_type=MESH)

    def take_turn(t):
        pl.semaphore_wait(token.at[0], 1)

    pl.semaphore_wait(barrier, PEERS + 4)
    on(0, (send, 0))

    for copy in load_adj:
        copy.start()
    load_held.wait()
    hand_on(0)
    load_weight.wait()
    pltpu.make_async_copy(adjacency, adjacency, adj_sem).wait()

    def mask(r, carry):
        lane = lax.broadcasted_iota(jnp.int32, (BLOCK, 2 * BLOCK), 1)
        for k in range(slots // 2):
            live = lane < (counts[r] - 2 * k) * BLOCK
            adjacency[r, k] = jnp.where(live, adjacency[r, k], jnp.zeros((), jnp.bfloat16))
        return carry

    lax.fori_loop(0, blocks, mask, 0)

    on(0, (give_way, 0))
    on(1, (take_turn, 0), (send, 0))
    on(1, (send, 1))
    first_half(0)
    hand_on(1)
    second_half(0)
    on(0, (hold_back, 1), (send, 1))

    @pl.when(section == 0)
    def _():
        send(2)

    first_half(1)
    hand_on(2)

    @pl.when((core == 0) & (section > 0))
    def _():
        send(2, (0, 1, 2))

    second_half(1)

    @pl.when((core == 0) & (section > 0))
    def _():
        send(2, (3,))

    hand_on(3)
    on(1, (send, 2), (send, 3))
    first_half(2)
    hand_on(4)
    second_half(2)
    on(0, (hold_back, 2), (send, 3))
    first_half(3)
    second_half(3)

    @pl.when(core == 1)
    def _():
        sent(0, 0).wait()

    for t, late in ((0, 1), (1, 0), (1, 1), (2, 0), (2, 1), (3, 0), (3, 1)):
        sent(t, late).wait()

    @pl.when(section < n_section - 1)
    def _():
        for t in range(STEPS - 1):
            pltpu.make_async_copy(result.at[t], result.at[t], ship_send.at[t]).wait()

    for n in range(len(hands)):

        @pl.when(hands[n])
        def _():
            hand(n).wait_send()


def solution(mesh):
    n_section, n_dom = mesh.shape["section"], mesh.shape["dom"]
    n_x = math.isqrt(n_dom)
    n_z = n_dom // n_x

    def body(carry_h, carry_h0, new_h0, weights, adj_blocks, col_index, counts, send_list):
        rows, width = carry_h.shape[1:]
        blocks, slots = adj_blocks.shape[:2]
        wide = width // CHUNKS
        tiles = (blocks, BLOCK, width)
        anywhere = pl.BlockSpec(memory_space=pltpu.HBM)
        scalars = pl.BlockSpec(memory_space=pltpu.SMEM)
        vmem = lambda *shape: pltpu.VMEM(shape, jnp.bfloat16)
        dma = lambda *shape: pltpu.SemaphoreType.DMA(shape)
        out = pl.pallas_call(
            functools.partial(kernel, n_section, n_x, n_z),
            out_shape=vmem(STEPS, *tiles),
            in_specs=[scalars] * 3 + [anywhere] * 5,
            out_specs=pl.BlockSpec(memory_space=pltpu.VMEM),
            scratch_shapes=[vmem(blocks, BLOCK, wide)] * (STEPS * CHUNKS)
            + [vmem(PER, blocks + n_dom, BLOCK, wide)] * (STEPS * HALVES)
            + [
                vmem(STEPS, CHUNKS, PEERS, BLOCK, wide),
                vmem(STEPS, *tiles),
                pltpu.VMEM((blocks // 2, 2 * BLOCK, width), jnp.float32),
                vmem(blocks // 2, 2 * BLOCK, width // HALVES),
                vmem(STEPS - 1, CHUNKS, blocks, BLOCK, wide),
                vmem(blocks, slots // 2, BLOCK, 2 * BLOCK),
                vmem(width, width),
                pltpu.SemaphoreType.REGULAR((3,)),
                dma(3),
                dma(2, STEPS - 1),
                pltpu.SemaphoreType.DMA,
                dma(STEPS, HALVES),
                dma(STEPS, 2),
                dma(STEPS, HALVES),
                dma(STEPS - 1),
                dma(STEPS - 1, CHUNKS),
                dma(5),
                dma(STEPS),
            ],
            compiler_params=pltpu.CompilerParams(
                collective_id=0, has_side_effects=True, vmem_limit_bytes=67_043_328 - (4 << 20) - (64 << 10)
            ),
        )(
            col_index, counts, send_list,
            carry_h.reshape(1, *tiles), carry_h0.reshape(1, *tiles), new_h0.reshape(-1, *tiles), weights, adj_blocks,
        )
        return out.reshape(1, STEPS, rows, width)

    in_specs = (
        P("section", "dom", None),
        P("section", "dom", None),
        P(None, "dom", None),
        P("section", None, None),
        P("dom", None, None, None),
        P("dom", None),
        P("dom"),
        P(),
    )
    out_specs = P("section", None, "dom", None)
    return jax.shard_map(body, mesh=mesh, in_specs=in_specs, out_specs=out_specs, check_vma=False)
```

```python
import functools
import math

import jax
import jax.numpy as jnp
from jax import lax
from jax.experimental import pallas as pl
from jax.experimental.pallas import tpu as pltpu
from jax.sharding import PartitionSpec as P

BLOCK = 128
STEPS = 4
TELEPORT = 0.2
STRENGTH = 1.5
MESH = pl.DeviceIdType.MESH
CHUNKS = 4
HALVES = 2
PER = CHUNKS // HALVES

ORDER = (
    (2, 2),
    (2, 1), (1, 2), (2, -1), (-1, 2),
    (1, 1), (-1, -1),
    (1, -1), (-1, 1),
    (2, 0), (0, 2),
    (1, 0), (-1, 0), (0, 1), (0, -1),
)
PEERS = len(ORDER)
FIRST = 3


def beta_at(layer):
    return math.log(1.0 + STRENGTH / (layer + 1))


def beta_of(section, n_section):
    value = jnp.float32(beta_at(n_section - 1))
    for s in range(n_section - 1):
        value = jnp.where(section == s, jnp.float32(beta_at(s)), value)
    return value


def mixture_of(col, table, adjacency, anchor, r):
    def entry(n):
        return jnp.concatenate([table[c, n] for c in range(PER)], axis=1)

    total = None
    for k in range(adjacency.shape[1]):
        picked = jnp.concatenate([entry(col[r, 2 * k]), entry(col[r, 2 * k + 1])], axis=0)
        term = jnp.dot(adjacency[r, k], picked, preferred_element_type=jnp.float32)
        total = term if total is None else total + term
    return ((1.0 - TELEPORT) * total + TELEPORT * anchor.astype(jnp.float32)).astype(jnp.bfloat16)


def layer_of(partial, right, weight, beta):
    half = right.shape[1]
    layer = partial + beta * jnp.dot(right, weight, preferred_element_type=jnp.float32)
    layer = jnp.concatenate([layer[:, :half], layer[:, half:] + (1.0 - beta) * right.astype(jnp.float32)], axis=1)
    return jnp.maximum(layer, 0.0).astype(jnp.bfloat16)


def by_pairs(pairs, lines, mix, use, after):
    def gather(g):
        lines[g] = jnp.concatenate([mix(2 * g), mix(2 * g + 1)], axis=0)

    def rows(g, carry):
        use(g - 1, lines[g - 1])
        gather(g)
        after(g - 1)
        return carry

    gather(0)
    lax.fori_loop(1, pairs, rows, 0)
    use(pairs - 1, lines[pairs - 1])
    after(pairs - 1)


def last_kernel(n_section, col, done, table, held, partial, adjacency, weight, out, lines, result, done_sem, out_sem):
    section = lax.axis_index("section")
    last, blocks = STEPS - 1, result.shape[0]
    half = lines.shape[2]
    beta = beta_of(section, n_section)

    def put(t):
        return pltpu.make_async_copy(done.at[t], out.at[t], done_sem.at[t])

    def leave(g):
        rows = pl.ds(2 * g, 2)
        return pltpu.make_async_copy(result.at[rows], out.at[last, rows], out_sem.at[g])

    for t in range(last):
        put(t).start()

    def mix(r):
        return mixture_of(col, table, adjacency, held[last, r, :, half:], r)

    def use(g, right):
        layer = layer_of(partial[g], right, weight[half:], beta)
        for i in range(2):
            result[2 * g + i] = layer[i * BLOCK : (i + 1) * BLOCK]

    by_pairs(blocks // 2, lines, mix, use, lambda g: leave(g).start())
    for t in range(last):
        put(t).wait()
    for g in range(blocks // 2):
        leave(g).wait()


def kernel(n_section, n_x, n_z, col, counts, send_list, carry_h, carry_h0, new_h0, weights, adj, out, last_table, held, partial, adjacency, weight, *scratch):
    owns, scratch = [scratch[t * CHUNKS : (t + 1) * CHUNKS] for t in range(STEPS)], scratch[STEPS * CHUNKS :]
    tables, scratch = [*scratch[: STEPS * HALVES - 1], last_table], scratch[STEPS * HALVES - 1 :]
    tables = [tables[t * HALVES : (t + 1) * HALVES] for t in range(STEPS)]
    (
        outgoing, lines, result,
        token, load_sem, feed_sem, adj_sem, own_sem, send_sem, recv_sem, ship_send, ship_recv, held_send, held_recv,
    ) = scratch
    section = lax.axis_index("section")
    part = lax.axis_index("dom")
    z, x = part // n_x, part % n_x
    core = section % 2
    blocks = held.shape[1]
    slots = adj.shape[1]
    wide = weight.shape[1] // CHUNKS
    half = PER * wide

    def at(dx, dz):
        return ((z + dz + n_z) % n_z) * n_x + (x + dx + n_x) % n_x

    def along(by):
        return {"section": (section + by + n_section) % n_section}

    barrier = pltpu.get_barrier_semaphore()
    for dx, dz in ORDER:
        pl.semaphore_signal(barrier, inc=1, device_id={"dom": at(dx, dz)}, device_id_type=MESH)
    for by in (1, -1, 2, -2):
        pl.semaphore_signal(barrier, inc=1, device_id=along(by), device_id_type=MESH)

    def columns(c):
        return pl.ds(c * wide, wide)

    def load_x(c):
        return pltpu.make_async_copy(carry_h.at[0, :, :, columns(c)], owns[0][c], load_sem.at[0])

    load_held = pltpu.make_async_copy(carry_h0.at[0], held.at[0], load_sem.at[1])
    load_weight = pltpu.make_async_copy(weights.at[0], weight, load_sem.at[2])
    for c in range(CHUNKS):
        load_x(c).start()
    load_held.start()
    load_weight.start()

    def feed_x(t, c):
        return pltpu.make_async_copy(new_h0.at[t - 1, :, :, columns(c)], owns[t][c], feed_sem.at[0, t - 1])

    def feed_held(t):
        return pltpu.make_async_copy(new_h0.at[t - 1], held.at[t], feed_sem.at[1, t - 1])

    @pl.when(section == 0)
    def _():
        for t in range(1, STEPS):
            for c in range(CHUNKS):
                feed_x(t, c).start()
            feed_held(t).start()

    load_adj = [
        pltpu.make_async_copy(
            adj.at[:, k], adjacency.at[:, k // 2, :, pl.ds((k % 2) * BLOCK, BLOCK)], adj_sem
        )
        for k in range(slots)
    ]

    def exchange(t, c, j, owner):
        dx, dz = ORDER[j]
        return pltpu.make_async_remote_copy(
            src_ref=outgoing.at[t, c, j],
            dst_ref=tables[t][c // PER].at[c % PER, blocks + owner],
            send_sem=send_sem.at[t, int(c >= FIRST)],
            recv_sem=recv_sem.at[t, c // PER],
            device_id={"dom": at(dx, dz)},
            device_id_type=MESH,
        )

    def sent(t, late):
        part_of = outgoing.at[t, pl.ds(FIRST, CHUNKS - FIRST) if late else pl.ds(0, FIRST)]
        return pltpu.make_async_copy(part_of, part_of, send_sem.at[t, late])

    def arrived(t, h):
        part_of = tables[t][h].at[:, pl.ds(blocks, PEERS)]
        return pltpu.make_async_copy(part_of, part_of, recv_sem.at[t, h])

    def own_done(t, h):
        part_of = tables[t][h].at[:, pl.ds(0, blocks)]
        return pltpu.make_async_copy(part_of, part_of, own_sem.at[t, h])

    def ship(t, c, first, count):
        rows = pl.ds(first, count)
        return pltpu.make_async_remote_copy(
            src_ref=result.at[t, c, rows],
            dst_ref=owns[t + 1][c].at[rows],
            send_sem=ship_send.at[t],
            recv_sem=ship_recv.at[t, c],
            device_id=along(1),
            device_id_type=MESH,
        )

    def hand(n):
        source, target, by = ((0, 1, 1), (0, 2, 2), (1, 2, 1), (1, 3, 2), (2, 3, 1))[n]
        return pltpu.make_async_remote_copy(
            src_ref=held.at[source],
            dst_ref=held.at[target],
            send_sem=held_send.at[n],
            recv_sem=held_recv.at[target],
            device_id=along(by),
            device_id_type=MESH,
        )

    hands = (
        section < n_section - 1,
        (core == 0) & (section < n_section - 2),
        core == 0,
        (core == 0) & (section < n_section - 2),
        core == 0,
    )

    def hand_on(n):
        @pl.when(hands[n])
        def _():
            hand(n).start()

    def own_to_table(t, c):
        return pltpu.make_async_copy(
            owns[t][c], tables[t][c // PER].at[c % PER, pl.ds(0, blocks)], own_sem.at[t, c // PER]
        )

    def send(t, chunks=range(CHUNKS)):
        if 0 not in chunks:
            pass
        elif t == 0:
            pltpu.make_async_copy(held.at[0], held.at[0], load_sem.at[0]).wait()
        else:

            @pl.when(section == 0)
            def _():
                pltpu.make_async_copy(held.at[t], held.at[t], feed_sem.at[0, t - 1]).wait()

        for c in chunks:
            if t:

                @pl.when(section > 0)
                def _():
                    ship(t - 1, c, 0, blocks).wait_recv()

            own_to_table(t, c).start()
            for j, (dx, dz) in enumerate(ORDER):
                outgoing[t, c, j] = owns[t][c][send_list[part, at(dx, dz)]]
                if j:
                    exchange(t, c, j - 1, part).start()
            tables[t][c // PER][c % PER, blocks + part] = owns[t][c][send_list[part, part]]
            exchange(t, c, PEERS - 1, part).start()

    def wait_held(t):
        if t == 0:
            load_held.wait()
        else:

            @pl.when(section == 0)
            def _():
                feed_held(t).wait()

            @pl.when(section > 0)
            def _():
                hand((0, 0, 1, 3)[t]).wait_recv()

    def wait_table(t, h):
        own_done(t, h).wait()
        arrived(t, h).wait()

    def mix(t, h, r):
        return mixture_of(col, tables[t][h], adjacency, held[t, r, :, h * half : (h + 1) * half], r)

    def pipelined(t, h, use, after=lambda g: None):
        by_pairs(blocks // 2, lines, lambda r: mix(t, h, r), use, after)

    def begin(t):
        beta = beta_of(section, n_section)

        def use(g, left):
            product = beta * jnp.dot(left, weight[:half], preferred_element_type=jnp.float32)
            partial[g, :, :half] = product[:, :half] + (1.0 - beta) * left.astype(jnp.float32)
            partial[g, :, half:] = product[:, half:]

        pipelined(t, 0, use)

    def finish(t):
        beta = beta_of(section, n_section)

        def use(g, right):
            layer = layer_of(partial[g], right, weight[half:], beta)
            for i in range(2):
                rows_of = layer[i * BLOCK : (i + 1) * BLOCK]
                out[t, 2 * g + i] = rows_of
                for c in range(CHUNKS):
                    result[t, c, 2 * g + i] = rows_of[:, c * wide : (c + 1) * wide]

        def after(g):
            if t < STEPS - 1:

                @pl.when(section < n_section - 1)
                def _():
                    ship(t, 0, 2 * g, 2).start()

        pipelined(t, 1, use, after)
        if t < STEPS - 1:

            @pl.when(section < n_section - 1)
            def _():
                for c in range(1, CHUNKS):
                    ship(t, c, 0, blocks).start()

    def let_in(n):
        @pl.when(section == 1)
        def _():
            pl.semaphore_signal(token.at[n], inc=1, device_id=along(-1), device_id_type=MESH)

    def first_half(t):
        if t:
            wait_held(t)
        wait_table(t, 0)
        if t == 1:
            let_in(1)
        begin(t)

    def second_half(t):
        wait_table(t, 1)
        if t == 2:
            let_in(2)
        if t < STEPS - 1:
            finish(t)

    def on(which, *work):
        @pl.when(core == which)
        def _():
            for step, t in work:
                step(t)

    def hold_back(n):
        @pl.when(section == 0)
        def _():
            pl.semaphore_wait(token.at[n], 1)

    def give_way(t):
        sent(0, 0).wait()
        pl.semaphore_signal(token.at[0], inc=1, device_id=along(1), device_id_type=MESH)

    def take_turn(t):
        pl.semaphore_wait(token.at[0], 1)

    pl.semaphore_wait(barrier, PEERS + 4)
    on(0, (send, 0))

    for copy in load_adj:
        copy.start()
    load_held.wait()
    hand_on(0)
    load_weight.wait()
    pltpu.make_async_copy(adjacency, adjacency, adj_sem).wait()

    def mask(r, carry):
        lane = lax.broadcasted_iota(jnp.int32, (BLOCK, 2 * BLOCK), 1)
        for k in range(slots // 2):
            live = lane < (counts[r] - 2 * k) * BLOCK
            adjacency[r, k] = jnp.where(live, adjacency[r, k], jnp.zeros((), jnp.bfloat16))
        return carry

    lax.fori_loop(0, blocks, mask, 0)

    on(0, (give_way, 0))
    on(1, (take_turn, 0), (send, 0))
    on(1, (send, 1))
    first_half(0)
    hand_on(1)
    second_half(0)
    on(0, (hold_back, 1), (send, 1))

    @pl.when(section == 0)
    def _():
        send(2)

    first_half(1)
    hand_on(2)

    @pl.when((core == 0) & (section > 0))
    def _():
        send(2, (0, 1, 2))

    second_half(1)

    @pl.when((core == 0) & (section > 0))
    def _():
        send(2, (3,))

    hand_on(3)
    on(1, (send, 2), (send, 3))
    first_half(2)
    hand_on(4)
    second_half(2)
    on(0, (hold_back, 2), (send, 3))
    first_half(3)
    second_half(3)

    @pl.when(core == 1)
    def _():
        sent(0, 0).wait()

    for t, late in ((0, 1), (1, 0), (1, 1), (2, 0), (2, 1), (3, 0), (3, 1)):
        sent(t, late).wait()

    @pl.when(section < n_section - 1)
    def _():
        for t in range(STEPS - 1):
            pltpu.make_async_copy(result.at[t], result.at[t], ship_send.at[t]).wait()

    for n in range(len(hands)):

        @pl.when(hands[n])
        def _():
            hand(n).wait_send()


def solution(mesh):
    n_section, n_dom = mesh.shape["section"], mesh.shape["dom"]
    n_x = math.isqrt(n_dom)
    n_z = n_dom // n_x

    def body(carry_h, carry_h0, new_h0, weights, adj_blocks, col_index, counts, send_list):
        rows, width = carry_h.shape[1:]
        blocks, slots = adj_blocks.shape[:2]
        wide = width // CHUNKS
        tiles = (blocks, BLOCK, width)
        anywhere = pl.BlockSpec(memory_space=pltpu.HBM)
        scalars = pl.BlockSpec(memory_space=pltpu.SMEM)
        vmem = lambda *shape: pltpu.VMEM(shape, jnp.bfloat16)
        dma = lambda *shape: pltpu.SemaphoreType.DMA(shape)
        inside = pl.BlockSpec(memory_space=pltpu.VMEM)
        pair_sums = pltpu.VMEM((blocks // 2, 2 * BLOCK, width), jnp.float32)
        kept = [
            vmem(STEPS - 1, *tiles),
            vmem(PER, blocks + n_dom, BLOCK, wide),
            vmem(STEPS, *tiles),
            pair_sums,
            vmem(blocks, slots // 2, BLOCK, 2 * BLOCK),
            vmem(width, width),
        ]
        lines = vmem(blocks // 2, 2 * BLOCK, width // HALVES)
        kept = pl.pallas_call(
            functools.partial(kernel, n_section, n_x, n_z),
            out_shape=kept,
            in_specs=[scalars] * 3 + [anywhere] * 5,
            out_specs=[inside] * len(kept),
            scratch_shapes=[vmem(blocks, BLOCK, wide)] * (STEPS * CHUNKS)
            + [vmem(PER, blocks + n_dom, BLOCK, wide)] * (STEPS * HALVES - 1)
            + [
                vmem(STEPS, CHUNKS, PEERS, BLOCK, wide),
                lines,
                vmem(STEPS - 1, CHUNKS, blocks, BLOCK, wide),
                pltpu.SemaphoreType.REGULAR((3,)),
                dma(3),
                dma(2, STEPS - 1),
                pltpu.SemaphoreType.DMA,
                dma(STEPS, HALVES),
                dma(STEPS, 2),
                dma(STEPS, HALVES),
                dma(STEPS - 1),
                dma(STEPS - 1, CHUNKS),
                dma(5),
                dma(STEPS),
            ],
            compiler_params=pltpu.CompilerParams(
                collective_id=0, has_side_effects=True, vmem_limit_bytes=67_043_328 - (17 << 20) - (64 << 10)
            ),
        )(
            col_index, counts, send_list,
            carry_h.reshape(1, *tiles), carry_h0.reshape(1, *tiles), new_h0.reshape(-1, *tiles), weights, adj_blocks,
        )
        out = pl.pallas_call(
            functools.partial(last_kernel, n_section),
            out_shape=jax.ShapeDtypeStruct((STEPS, *tiles), jnp.bfloat16),
            in_specs=[scalars] + [inside] * len(kept),
            out_specs=anywhere,
            scratch_shapes=[lines, vmem(*tiles), dma(STEPS - 1), dma(blocks // 2)],
            compiler_params=pltpu.CompilerParams(vmem_limit_bytes=8 << 20),
        )(col_index, *kept)
        return out.reshape(1, STEPS, rows, width)

    in_specs = (
        P("section", "dom", None),
        P("section", "dom", None),
        P(None, "dom", None),
        P("section", None, None),
        P("dom", None, None, None),
        P("dom", None),
        P("dom"),
        P(),
    )
    out_specs = P("section", None, "dom", None)
    return jax.shard_map(body, mesh=mesh, in_specs=in_specs, out_specs=out_specs, check_vma=False)
```
